768 devices in a mesh: orb: 64 (over y, z_hi, core), dom: 12 (over z_lo, x).
Axes of the slice: x: 4, y: 8, z: 12 (z_hi: 4, z_lo: 3; z = z_hi * 3 + z_lo), core: 2. Of those that a mesh axis runs over, the one named last changes fastest.
Arguments:
- psi: float32 [2, 64, 96, 16, 128], P(None, 'orb', 'dom'), may hold values from -6 to 6
- occupations: float32 [64], P('orb'), may hold values from 0.5 to 2
- core_density: float32 [96, 16, 128], P('dom'), may hold values from 0.1 to 0.5
- external: float32 [96, 16, 128], P('dom'), may hold values from -3 to 3
Outputs:
- psi_next: float32 [2, 64, 96, 16, 128], P(None, 'orb', 'dom')
- v_mid: float32 [96, 16, 128], P('dom')
The draws below stay inside these ranges and needn't reach their ends.
All inputs are finite; a program needn't handle non-finite values.
Results may differ from the reference program's by a relative error of at most 0.00021.
Values sent between devices are 32-bit elements; how exact they have to be, the bound alone decides.
A program may use at most 32 MiB of HBM per device.

```python
import math
import jax
import jax.numpy as jnp
from jax import lax

NY = 16
NZ = 128
ORBS = 64
NX = 96


def draw_psi(key, part):
    key_level, key_flip, key_rough = jax.random.split(jax.random.fold_in(key, 11), 3)
    magnitude = jax.random.uniform(key_level, (2, ORBS, NX), jnp.float32, 2.0, 4.0)
    roughness = 0.35 * jax.random.normal(key_rough, (2, ORBS, NX, NY, NZ), jnp.float32)
    sign_flip = jnp.where(jax.random.bernoulli(key_flip, 0.5, (2, ORBS, NX)), 1.0, -1.0).astype(jnp.float32)
    layers = (magnitude * sign_flip)[:, :, :, None, None]
    return jnp.clip(layers + roughness, -6.0, 6.0).astype(jnp.float32)


def draw_external(key, part):
    key_level, key_flip, key_rough = jax.random.split(jax.random.fold_in(key, 23), 3)
    magnitude = jax.random.uniform(key_level, (NX,), jnp.float32, 2.0, 2.6)
    roughness = 0.3 * jax.random.normal(key_rough, (NX, NY, NZ), jnp.float32)
    sign_flip = jnp.where(jax.random.bernoulli(key_flip, 0.5, (NX,)), 1.0, -1.0).astype(jnp.float32)
    layers = (magnitude * sign_flip)[:, None, None]
    return jnp.clip(layers + roughness, -3.0, 3.0).astype(jnp.float32)


def steps_of(stream_key, shape, shards, least, largest):
    factor_of = 1.0
    for position, blocks in shards:
        heights = jax.random.uniform(jax.random.fold_in(jax.random.fold_in(stream_key, 6), position), (blocks,), jnp.float32, least / len(shards), largest / len(shards))
        factor_of = factor_of * jnp.repeat(jnp.exp(heights), shape[position] // blocks).reshape((-1,) + (1,) * (len(shape) - 1 - position))
    return factor_of


def setup_inputs(seed: int = 0) -> dict:
    arg_keys = jax.random.split(jax.random.key(seed), 5)
    psi = draw_psi(jax.random.fold_in(arg_keys[4], 71), 0)
    occupations = jnp.clip(jnp.exp(math.log(2.0) - 1.3862944 * jax.random.uniform(arg_keys[1], (ORBS,), jnp.float32) ** steps_of(arg_keys[1], (ORBS,), ((0, 64),), -0.2, 0.2)), 0.5, 2.0)
    core_density = jnp.clip(0.1 + 0.4 * jax.random.uniform(arg_keys[2], (NX, NY, NZ), jnp.float32) ** steps_of(arg_keys[2], (NX, NY, NZ), ((0, 12),), -0.2, 0.2), 0.1, 0.5)
    external = draw_external(jax.random.fold_in(arg_keys[4], 71), 0)
    return dict(psi=psi, occupations=occupations, core_density=core_density, external=external)


coeff_zero = -2.5
coeff_one = 4.0 / 3.0
coeff_two = -1.0 / 12.0
time_step = 0.5
exch_coeff = -((3.0 / math.pi) ** (1.0 / 3.0))


def second(field, axis):
    near = jnp.roll(field, 1, axis) + jnp.roll(field, -1, axis)
    far = jnp.roll(field, 2, axis) + jnp.roll(field, -2, axis)
    return coeff_zero * field + coeff_one * near + coeff_two * far


def hamilton(field, potential):
    lap = second(field, 1) + second(field, 2) + second(field, 3)
    return -0.5 * lap + potential[None] * field


def taylor(potential, orbital):
    total = orbital
    term = orbital
    for order in range(1, 5):
        image = hamilton(term, potential)
        term = jnp.stack([time_step * image[1] / order, -time_step * image[0] / order])
        total = total + term
    return total


def exchange_potential(orbitals, occupations, core_density):
    squares = orbitals[0] * orbitals[0] + orbitals[1] * orbitals[1]
    summed = jnp.tensordot(occupations, squares, axes=1, precision=lax.Precision.HIGHEST)
    density = core_density + summed / ORBS
    return exch_coeff * jnp.cbrt(density)


def propagate(potential, orbitals):
    moved = lax.map(lambda one: taylor(potential, one), jnp.swapaxes(orbitals, 0, 1))
    return jnp.swapaxes(moved, 0, 1)


def reference(psi, occupations, core_density, external):
    vx_start = exchange_potential(psi, occupations, core_density)
    v_start = external + vx_start
    psi_pred = propagate(v_start, psi)
    vx_pred = exchange_potential(psi_pred, occupations, core_density)
    v_mid = external + 0.5 * (vx_start + vx_pred)
    psi_next = propagate(v_mid, psi)
    return psi_next, v_mid
```

```python
import math

import jax
import jax.numpy as jnp
from jax import lax
from jax.experimental import pallas as pl
from jax.experimental.pallas import tpu as pltpu
from jax.sharding import PartitionSpec as P

time_step = 0.5
exch_coeff = -((3.0 / math.pi) ** (1.0 / 3.0))
MESH = pl.DeviceIdType.MESH

NYR, NZR, NCORE, NDOM, ORBS = 8, 4, 2, 12, 64
LAYERS, ROWS, HALF, LANES = 8, 16, 8, 128

Y_FAR = (4, 3, 5, 2, 6, 1, 7)
Y_NEAR = Y_FAR[::-1]
Z_OFFS = tuple((dd, dz) for dz in (2, 1, 3, 0) for dd in (-1, 1, 0) if (dd, dz) != (0, 0))
CHUNKS = {
    1: ((2, 2), (4, 4), (8, 4), (12, 4), (16, 4), (20, 2)),
    2: ((4, 4), (8, 4), (12, 4), (16, 4)),
    3: ((6, 2), (8, 4), (12, 4), (16, 2)),
    4: ((8, 4), (12, 4)),
}


def code(dd):
    return (0, 1, 2)[dd]


def z_slot(dd, dz):
    return code(dd) * NZR + dz


def stencil(ref, comp, first, count):
    field = ref[comp, first - 2 : first + count + 2]
    mid = field[2 : count + 2]
    near = field[1 : count + 1] + field[3 : count + 3]
    far = field[0:count] + field[4 : count + 4]
    near = near + (pltpu.roll(mid, 1, 1) + pltpu.roll(mid, ROWS - 1, 1))
    far = far + (pltpu.roll(mid, 2, 1) + pltpu.roll(mid, ROWS - 2, 1))
    near = near + (pltpu.roll(mid, 1, 2) + pltpu.roll(mid, LANES - 1, 2))
    far = far + (pltpu.roll(mid, 2, 2) + pltpu.roll(mid, LANES - 2, 2))
    return mid, near, far


def exchange_term(density):
    return exch_coeff * jnp.exp(jnp.log(density) * (1.0 / 3.0))


def kernel(
    occ_ref, psi_hbm, core_hbm, ext_hbm, psi_out, vmid_out,
    padded, lap1, t1, t2, t3, result, slabs, vx0, dens, dens_in, pair, y_in, z_in, vslab, pot,
    load_sem, halo_s, halo_r, slab_s, slab_r, pair_s, pair_r, y_s, y_r, z_s, z_r, g_s, g_r, f_s, f_r, out_sem,
):
    d = lax.axis_index("dom")
    o = lax.axis_index("orb")
    y = lax.div(o, NZR * NCORE)
    z = lax.rem(lax.div(o, NCORE), NZR)
    c = lax.rem(o, NCORE)
    other = 1 - c

    def peer(dd=0, dy=0, dz=0, dc=0):
        y2 = lax.rem(y + dy, NYR)
        z2 = lax.rem(z + dz, NZR)
        c2 = other if dc else c
        return {"dom": lax.rem(d + dd + NDOM, NDOM), "orb": (y2 * NZR + z2) * NCORE + c2}

    def remote(src, dst, send, recv, target):
        return pltpu.make_async_remote_copy(
            src_ref=src, dst_ref=dst, send_sem=send, recv_sem=recv, device_id=target, device_id_type=MESH
        )

    mine = pl.ds(pl.multiple_of(c * HALF, HALF), HALF)
    theirs = pl.ds(pl.multiple_of(other * HALF, HALF), HALF)
    centre = pl.ds(LAYERS, LAYERS)

    load_psi = pltpu.make_async_copy(psi_hbm, padded.at[:, centre], load_sem.at[0])
    load_core = pltpu.make_async_copy(core_hbm.at[y, mine], slabs.at[0, 0], load_sem.at[1])
    load_ext = pltpu.make_async_copy(ext_hbm.at[y, mine], slabs.at[0, 1], load_sem.at[2])
    load_psi.start()
    load_core.start()
    load_ext.start()

    barrier = pltpu.get_barrier_semaphore()
    partners = [peer(dc=1)] + [peer(dy=k) for k in Y_FAR] + [peer(dd=a, dz=b) for a, b in Z_OFFS]
    for target in partners:
        pl.semaphore_signal(barrier, inc=1, device_id=target, device_id_type=MESH)

    occ = occ_ref[0]
    waits = []

    def put_density(r, first, count, re, im):
        value = occ * (re * re + im * im)
        dens[r, 0, first : first + count] = value[:, :HALF]
        dens[r, 1, first : first + count] = value[:, HALF:]

    def reduce_to_slab(r, after_y_sent):
        swap = remote(dens.at[r, other], dens_in.at[r], pair_s.at[r], pair_r.at[r], peer(dc=1))
        swap.start()
        swap.wait_recv()
        waits.append(swap)
        pair[r] = dens[r, c] + dens_in[r]
        copies = {}
        for k in Y_FAR:
            y2 = lax.rem(y + k, NYR)
            copies[k] = remote(
                pair.at[r, y2], y_in.at[r, k - 1], y_s.at[r, k - 1], y_r.at[r, k - 1], peer(dy=k)
            )
            copies[k].start()
        after_y_sent()
        total = pair[r, y]
        for k in Y_NEAR:
            copies[k].wait_recv()
            total = total + y_in[r, k - 1]
        waits.extend(copies.values())
        z_in[r, 0] = total
        copies = {}
        for dd, dz in Z_OFFS:
            slot = z_slot(dd, dz)
            copies[dd, dz] = remote(
                z_in.at[r, 0], z_in.at[r, slot], z_s.at[r, slot], z_r.at[r, slot], peer(dd=dd, dz=dz)
            )
            copies[dd, dz].start()
        return copies

    def finish_slab(r, copies):
        for key in reversed(Z_OFFS):
            copies[key].wait_recv()
        waits.extend(copies.values())
        found = []
        for dd in (1, 0, -1):
            base = code(dd) * NZR
            summed = (z_in[r, base] + z_in[r, base + 2]) + (z_in[r, base + 1] + z_in[r, base + 3])
            found.append(exchange_term(slabs[code(dd), 0] + summed * (1.0 / ORBS)))
        return found

    def gather(r, while_waiting):
        pot[r, :, y, mine] = vslab[r]
        copies = {}
        for k in Y_FAR:
            copies[k] = remote(
                vslab.at[r], pot.at[r, :, y, mine], g_s.at[r, k - 1], g_r.at[r, k - 1], peer(dy=k)
            )
            copies[k].start()
        forwards = []

        def forward(k):
            layer = lax.rem(y + NYR - k, NYR)
            copy = remote(
                pot.at[r, :, layer, mine], pot.at[r, :, layer, mine], f_s.at[r, k], f_r.at[r, k], peer(dc=1)
            )
            copy.start()
            forwards.append(copy)

        forward(0)
        while_waiting()
        for k in Y_NEAR:
            copies[k].wait_recv()
            forward(k)
        for copy in forwards:
            copy.wait_recv()
        waits.extend(copies.values())
        waits.extend(forwards)

    def local_pot(r, first, count):
        block, offset = divmod(first, LAYERS)
        return pot[r, block, offset : offset + count]

    def first_order():
        for comp in range(2):
            for first, count in CHUNKS[1]:
                mid, near, far = stencil(padded, comp, first, count)
                lap1[comp, first : first + count] = 3.75 * mid - (2.0 / 3.0) * near + (1.0 / 24.0) * far

    def propagate(r, emit):
        for first, count in CHUNKS[1]:
            there = slice(first, first + count)
            v = local_pot(r, first, count)
            step = time_step
            t1[0, there] = step * (lap1[1, there] + v * padded[1, there])
            t1[1, there] = -step * (lap1[0, there] + v * padded[0, there])
        for order, src, dst in ((2, t1, t2), (3, t2, t3)):
            step = time_step / order
            for first, count in CHUNKS[order]:
                there = slice(first, first + count)
                v = step * local_pot(r, first, count) + step * 3.75
                mid, near, far = stencil(src, 1, first, count)
                dst[0, there] = v * mid - (step * 2.0 / 3.0) * near + (step / 24.0) * far
                mid, near, far = stencil(src, 0, first, count)
                dst[1, there] = (step * 2.0 / 3.0) * near - v * mid - (step / 24.0) * far
        step = time_step / 4
        for first, count in CHUNKS[4]:
            there = slice(first, first + count)
            v = step * local_pot(r, first, count) + step * 3.75
            mid, near, far = stencil(t3, 1, first, count)
            re = v * mid - (step * 2.0 / 3.0) * near + (step / 24.0) * far
            re = re + ((padded[0, there] + t1[0, there]) + (t2[0, there] + t3[0, there]))
            mid, near, far = stencil(t3, 0, first, count)
            im = (step * 2.0 / 3.0) * near - v * mid - (step / 24.0) * far
            im = im + ((padded[1, there] + t1[1, there]) + (t2[1, there] + t3[1, there]))
            emit(first - LAYERS, count, re, im)

    load_psi.wait()
    for first in (0, 4):
        there = pl.ds(LAYERS + first, 4)
        put_density(0, first, 4, padded[0, there], padded[1, there])
    load_core.wait()
    load_ext.wait()
    pl.semaphore_wait(barrier, len(partners))

    halo = {
        1: remote(padded.at[:, centre], padded.at[:, pl.ds(0, LAYERS)], halo_s.at[0], halo_r.at[0], peer(dd=1)),
        -1: remote(
            padded.at[:, centre], padded.at[:, pl.ds(2 * LAYERS, LAYERS)], halo_s.at[1], halo_r.at[1], peer(dd=-1)
        ),
    }
    slab_copies = [
        remote(slabs.at[0], slabs.at[code(dd)], slab_s.at[code(dd)], slab_r.at[code(dd)], peer(dd=dd))
        for dd in (1, -1)
    ]

    def send_halo():
        for copy in slab_copies:
            copy.start()
        for copy in halo.values():
            copy.start()

    def nothing():
        pass

    sent = reduce_to_slab(0, send_halo)
    for copy in slab_copies:
        copy.wait_recv()
    waits.extend(slab_copies)
    for index, value in enumerate(finish_slab(0, sent)):
        slot = (1, 0, 2)[index]
        vx0[index] = value
        vslab[0, index] = slabs[slot, 1] + value

    def wait_halo():
        for copy in halo.values():
            copy.wait_recv()
        waits.extend(halo.values())
        first_order()

    gather(0, wait_halo)
    propagate(0, lambda first, count, re, im: put_density(1, first, count, re, im))

    sent = reduce_to_slab(1, nothing)
    for index, value in enumerate(finish_slab(1, sent)):
        slot = (1, 0, 2)[index]
        vslab[1, index] = slabs[slot, 1] + 0.5 * (vx0[index] + value)
    gather(1, nothing)

    store_pot = pltpu.make_async_copy(pot.at[1, 1], vmid_out, out_sem.at[0])
    store_pot.start()
    stores = [store_pot]

    def emit_result(first, count, re, im):
        there = slice(first, first + count)
        result[0, there] = re
        result[1, there] = im
        copy = pltpu.make_async_copy(
            result.at[:, pl.ds(first, count)], psi_out.at[:, pl.ds(first, count)], out_sem.at[1 + first // 4]
        )
        copy.start()
        stores.append(copy)

    propagate(1, emit_result)
    for copy in waits:
        copy.wait_send()
    for copy in stores:
        copy.wait()


def shards(psi, occupations, core_density, external):
    f32 = jnp.float32
    dma = pltpu.SemaphoreType.DMA
    brick = (2, LAYERS, ROWS, LANES)
    wide = (2, 3 * LAYERS, ROWS, LANES)
    tile = (HALF, LANES)
    anywhere = pl.BlockSpec(memory_space=pl.ANY)
    psi_next, v_mid = pl.pallas_call(
        kernel,
        out_shape=(jax.ShapeDtypeStruct(brick, f32), jax.ShapeDtypeStruct(core_density.shape, f32)),
        in_specs=[pl.BlockSpec(memory_space=pltpu.SMEM), anywhere, anywhere, anywhere],
        out_specs=(anywhere, anywhere),
        scratch_shapes=[
            pltpu.VMEM(wide, f32),
            pltpu.VMEM(wide, f32),
            pltpu.VMEM(wide, f32),
            pltpu.VMEM(wide, f32),
            pltpu.VMEM(wide, f32),
            pltpu.VMEM(brick, f32),
            pltpu.VMEM((3, 2, *tile), f32),
            pltpu.VMEM((3, *tile), f32),
            pltpu.VMEM((2, 2, LAYERS, *tile), f32),
            pltpu.VMEM((2, LAYERS, *tile), f32),
            pltpu.VMEM((2, LAYERS, *tile), f32),
            pltpu.VMEM((2, 7, *tile), f32),
            pltpu.VMEM((2, 12, *tile), f32),
            pltpu.VMEM((2, 3, *tile), f32),
            pltpu.VMEM((2, 3, LAYERS, ROWS, LANES), f32),
            dma((3,)), dma((2,)), dma((2,)), dma((3,)), dma((3,)), dma((2,)), dma((2,)), dma((2, 7)), dma((2, 7)),
            dma((2, 12)), dma((2, 12)), dma((2, 7)), dma((2, 7)), dma((2, 8)), dma((2, 8)), dma((3,)),
        ],
        compiler_params=pltpu.CompilerParams(collective_id=0, has_side_effects=True),
    )(occupations, psi.reshape(brick), core_density, external)
    return psi_next.reshape(psi.shape), v_mid


def solution(mesh):
    in_specs = (
        P(None, "orb", "dom", None, None),
        P("orb"),
        P("dom", None, None),
        P("dom", None, None),
    )
    out_specs = (P(None, "orb", "dom", None, None), P("dom", None, None))
    return jax.shard_map(shards, mesh=mesh, in_specs=in_specs, out_specs=out_specs, check_vma=False)
```
